32 devices in a mesh: fsdp: 8 (over y, x, core), rep: 4 (over z).
Axes of the slice: x: 2, y: 2, z: 4, core: 2. Of those that a mesh axis runs over, the one named last changes fastest.
Arguments:
- frames: bfloat16 [32, 1024, 768], P(('fsdp', 'rep')), may hold values from -6 to 6
- tokens: bfloat16 [32, 448, 768], P(('fsdp', 'rep')), may hold values from -6 to 6
- memory: bfloat16 [32, 1024, 768], P(('fsdp', 'rep')), may hold values from -6 to 6
- segment_ids: int32 [32, 448], P(('fsdp', 'rep')), may hold values from 0 to 3, never falling along the last dimension, each value on 1 to 224 neighbouring positions
- enc_attn: float32 [4, 768, 768], P(None, ('fsdp', 'rep')), may hold values from -1 to 1
- enc_up: float32 [768, 3072], P(('fsdp', 'rep')), may hold values from -0.21875 to 0.21875
- enc_down: float32 [3072, 768], P(('fsdp', 'rep')), may hold values from -0.109375 to 0.109375
- enc_vec: float32 [8, 768], P(None, ('fsdp', 'rep')), may hold values from -1.2 to 1.4
- enc_up_bias: float32 [3072], P(('fsdp', 'rep')), may hold values from -1.2 to 1.2
- dec_attn: float32 [8, 768, 768], P(None, ('fsdp', 'rep')), may hold values from -1 to 1
- dec_up: float32 [768, 3072], P(('fsdp', 'rep')), may hold values from -0.21875 to 0.21875
- dec_down: float32 [3072, 768], P(('fsdp', 'rep')), may hold values from -0.109375 to 0.109375
- dec_vec: float32 [12, 768], P(None, ('fsdp', 'rep')), may hold values from -1.2 to 1.4
- dec_up_bias: float32 [3072], P(('fsdp', 'rep')), may hold values from -1.2 to 1.2
- dec_down_bias: float32 [768], P(('fsdp', 'rep')), may hold values from -1.2 to 1.2
- enc_out_grad: float32 [32, 1024, 768], P(('fsdp', 'rep')), may hold values from -6 to 6
- dec_out_grad: float32 [32, 448, 768], P(('fsdp', 'rep')), may hold values from -6 to 6
Outputs:
- enc_out: float32 [32, 1024, 768], P(('fsdp', 'rep'))
- dec_out: float32 [32, 448, 768], P(('fsdp', 'rep'))
- frames_grad: float32 [32, 1024, 768], P(('fsdp', 'rep'))
- tokens_grad: float32 [32, 448, 768], P(('fsdp', 'rep'))
- memory_grad: float32 [32, 1024, 768], P(('fsdp', 'rep'))
- enc_attn_grad: float32 [4, 768, 768], P(None, ('fsdp', 'rep'))
- enc_up_grad: float32 [768, 3072], P(('fsdp', 'rep'))
- enc_down_grad: float32 [3072, 768], P(('fsdp', 'rep'))
- enc_vec_grad: float32 [8, 768], P(None, ('fsdp', 'rep'))
- enc_up_bias_grad: float32 [3072], P(('fsdp', 'rep'))
- dec_attn_grad: float32 [8, 768, 768], P(None, ('fsdp', 'rep'))
- dec_up_grad: float32 [768, 3072], P(('fsdp', 'rep'))
- dec_down_grad: float32 [3072, 768], P(('fsdp', 'rep'))
- dec_vec_grad: float32 [12, 768], P(None, ('fsdp', 'rep'))
- dec_up_bias_grad: float32 [3072], P(('fsdp', 'rep'))
- dec_down_bias_grad: float32 [768], P(('fsdp', 'rep'))
The draws below stay inside these ranges and needn't reach their ends.
Inputs may be any that keep to these rules, and one draw needn't show every extreme that they name: `segment_ids`: along each row the ids never fall; each of the 4 transcripts holds 1 to 224 tokens, and one holds exactly that many.
All inputs are finite; a program needn't handle non-finite values.
Results may differ from the reference program's by a relative error of at most 0.025.
The reference program's roundings to bfloat16 on the way count: a program that leaves them out, or rounds other values in their place, can miss the bound.
Values may be sent and summed in bfloat16 or wider, within the bound.
A program may use at most 320 MiB of HBM per device.

```python
import math
import jax
import jax.numpy as jnp
import numpy as np
from jax import lax

D = 768
HEADS = 12
HEAD_DIM = 64
FF = 3072
FRAMES = 1024
DEC_LEN = 448
SEGMENTS = 4
CLIPS = 32


def attention_stack(key, slot_scales):
    values = jax.random.truncated_normal(key, -4.0, 4.0, (len(slot_scales), D, D), jnp.float32)
    factor = jnp.array(slot_scales, jnp.float32) * D ** (-0.5)
    return values * factor[:, None, None]


def draw_enc_attn(key, part):
    return attention_stack(jax.random.fold_in(key, 11), [2.0, 1.0, 1.0, 4.0])


def draw_dec_attn(key, part):
    return attention_stack(jax.random.fold_in(key, 13), [2.0, 1.0, 1.0, 2.0, 2.0, 1.0, 1.0, 4.0])


def vector_table(key, gain_rows, row_count):
    key_gain, key_shift = jax.random.split(key)
    gain_values = jax.random.uniform(key_gain, (row_count, D), jnp.float32, 0.6, 1.4)
    shift_values = 0.3 * jax.random.truncated_normal(key_shift, -4.0, 4.0, (row_count, D), jnp.float32)
    gain_mask = jnp.array([slot_index in gain_rows for slot_index in range(row_count)])
    return jnp.where(gain_mask[:, None], gain_values, shift_values)


def draw_enc_vec(key, part):
    return vector_table(jax.random.fold_in(key, 17), [0, 5], 8)


def draw_dec_vec(key, part):
    return vector_table(jax.random.fold_in(key, 19), [0, 5, 10], 12)


def with_spikes(values, key, source, target, parts, factor):
    def block_of(position):
        return (jnp.arange(values.shape[position]) // (values.shape[position] // parts)).reshape((-1,) + (1,) * (values.ndim - 1 - position))

    one_side = jax.random.permutation(key, parts)[block_of(target)]
    other_side = (block_of(target) + parts // 2) % parts
    return jnp.where((block_of(source) == one_side) | (block_of(source) == other_side), factor * values, values)


def steps_of(stream_key, shape, cuts, least, high):
    def one(dim, shards_of):
        draws = jax.random.uniform(jax.random.fold_in(jax.random.fold_in(stream_key, 6), dim), (shards_of,), jnp.float32, least / len(cuts), high / len(cuts))
        return jnp.repeat(jnp.exp(draws), shape[dim] // shards_of).reshape((-1,) + (1,) * (len(shape) - dim - 1))

    factor_of = one(*cuts[0])
    for cut in cuts[1:]:
        factor_of = factor_of * one(*cut)
    return factor_of


def length_profile(amount, total, most, lean):
    portions = [(1 << 20) // math.isqrt(rank ** lean) + 1 for rank in range(2, amount + 1)]
    spare, holding = total - most - (amount - 1), [1] * (amount - 1)
    while spare > 0:
        movable = [i for i in range(amount - 1) if holding[i] < most]
        pool, budget = sum([portions[i] for i in movable]), spare
        for i in movable:
            more = min(most - holding[i], max(1, budget * portions[i] // pool), spare)
            holding[i] = holding[i] + more
            spare = spare - more
    return np.array([most] + holding)


def uneven_parts(own_key, count, total, limit, skew):
    if count == 2:
        one = jax.random.randint(own_key, (), max(1, total - limit), min(limit, total - 1) + 1)
        return jnp.stack([one, total - one])
    tallies = jnp.asarray(length_profile(count, total, limit, skew), jnp.int32)
    couples = (count - 1) // 2
    giver, sink = tallies[1:1 + 2 * couples:2], tallies[2:2 + 2 * couples:2]
    margin = jnp.minimum(giver - 1, limit - sink)
    shifted = jax.random.randint(jax.random.fold_in(own_key, 1), (couples,), 0, 1 << 20) % (margin + 1)
    tallies = tallies.at[1:1 + 2 * couples:2].set(giver - shifted).at[2:2 + 2 * couples:2].set(sink + shifted)
    return tallies[jax.random.permutation(jax.random.fold_in(own_key, 2), count)]


def scatter_about(key, dims, scale, most, pieces=(), held_as=jnp.bfloat16):
    values = scale * jax.random.normal(key, dims, jnp.float32)
    if pieces:
        values = values * steps_of(key, dims, pieces, -0.22, 0.18)
    return jnp.clip(values, -most, most).astype(held_as)


def bell_draw_with(key, shape, width, limit, pieces, heavy, kind=jnp.bfloat16):
    entries = width * jax.random.normal(key, shape, jnp.float32)
    if pieces:
        entries = entries * steps_of(key, shape, pieces, -0.22, 0.18)
    return jnp.clip(with_spikes(entries, jax.random.fold_in(key, 3), *heavy), -limit, limit).astype(kind)


def setup_inputs(seed: int = 0) -> dict:
    seeds = jax.random.split(jax.random.key(seed), 18)
    frames = scatter_about(seeds[0], (CLIPS, FRAMES, D), 1.0, 6.0, ((0, 32),))
    tokens = scatter_about(seeds[1], (CLIPS, DEC_LEN, D), 1.0, 6.0, ((0, 32),))
    memory = scatter_about(seeds[2], (CLIPS, FRAMES, D), 1.0, 6.0, ((0, 32),))
    segment_ids = jax.vmap(lambda own: jnp.searchsorted(jnp.cumsum(uneven_parts(own, SEGMENTS, DEC_LEN, DEC_LEN // 2, 1)), jnp.arange(DEC_LEN), side="right"))(jax.random.split(seeds[3], CLIPS)).reshape((CLIPS, DEC_LEN)).astype(jnp.int32)
    enc_attn = draw_enc_attn(jax.random.fold_in(seeds[17], 71), 0)
    enc_up = scatter_about(seeds[5], (D, FF), D ** -0.5, 0.21875, ((0, 32),), jnp.float32)
    enc_down = scatter_about(seeds[6], (FF, D), FF ** -0.5, 0.109375, ((0, 32),), jnp.float32)
    enc_vec = draw_enc_vec(jax.random.fold_in(seeds[17], 71), 0)
    enc_up_bias = scatter_about(seeds[8], (FF,), 0.3, 1.2, ((0, 32),), jnp.float32)
    dec_attn = draw_dec_attn(jax.random.fold_in(seeds[17], 71), 0)
    dec_up = scatter_about(seeds[10], (D, FF), D ** -0.5, 0.21875, ((0, 32),), jnp.float32)
    dec_down = scatter_about(seeds[11], (FF, D), FF ** -0.5, 0.109375, ((0, 32),), jnp.float32)
    dec_vec = draw_dec_vec(jax.random.fold_in(seeds[17], 71), 0)
    dec_up_bias = scatter_about(seeds[13], (FF,), 0.3, 1.2, ((0, 32),), jnp.float32)
    dec_down_bias = scatter_about(seeds[14], (D,), 0.3, 1.2, ((0, 32),), jnp.float32)
    enc_out_grad = bell_draw_with(seeds[15], (CLIPS, FRAMES, D), 1.0, 6.0, ((0, 32),), (0, 2, 32, 2.75), jnp.float32)
    dec_out_grad = bell_draw_with(seeds[16], (CLIPS, DEC_LEN, D), 1.0, 6.0, ((0, 32),), (0, 2, 32, 2.75), jnp.float32)
    return {"frames": frames, "tokens": tokens, "memory": memory, "segment_ids": segment_ids, "enc_attn": enc_attn, "enc_up": enc_up, "enc_down": enc_down, "enc_vec": enc_vec, "enc_up_bias": enc_up_bias, "dec_attn": dec_attn, "dec_up": dec_up, "dec_down": dec_down, "dec_vec": dec_vec, "dec_up_bias": dec_up_bias, "dec_down_bias": dec_down_bias, "enc_out_grad": enc_out_grad, "dec_out_grad": dec_out_grad}


@jax.custom_vjp
def low(v):
    return lax.optimization_barrier(v.astype(jnp.bfloat16)).astype(jnp.float32)

@jax.custom_vjp
def low_back(v):
    return v

def low_keep(v):
    return (low(v), None)

def low_pass(kept, grad):
    return (grad,)

def back_keep(v):
    return (v, None)

def back_low(kept, grad):
    return (low(grad),)
low.defvjp(low_keep, low_pass)
low_back.defvjp(back_keep, back_low)
highest = lax.Precision.HIGHEST
epsilon = 1e-05
masked_score = -1e+30

def matmul(left, right):
    return jnp.dot(left, right, precision=highest, preferred_element_type=jnp.float32)

def layer_norm(inputs, gain, shift):
    center = inputs - lax.optimization_barrier(jnp.mean(inputs, -1, keepdims=True))
    spread = lax.optimization_barrier(jnp.mean(center * center, -1, keepdims=True))
    return center * lax.rsqrt(spread + epsilon) * gain + shift

def attend(queries, keys_in, values_in, segment_row, causal):
    row_count = queries.shape[0]
    block_rows = min(512, row_count)
    key_heads = keys_in.reshape(-1, HEADS, HEAD_DIM)
    value_heads = values_in.reshape(-1, HEADS, HEAD_DIM)
    key_index = jnp.arange(keys_in.shape[0], dtype=jnp.int32)

    def one_block(block_index):
        first_row = block_index * block_rows
        query_block = lax.dynamic_slice_in_dim(queries, first_row, block_rows, 0).reshape(block_rows, HEADS, HEAD_DIM)
        scores = jnp.einsum('qhd,khd->hqk', query_block, key_heads, precision=highest)
        scores = low_back(scores)
        if causal:
            query_index = first_row + jnp.arange(block_rows, dtype=jnp.int32)
            query_segment = lax.dynamic_slice_in_dim(segment_row, first_row, block_rows, 0)
            allowed = (query_segment[:, None] == segment_row[None, :]) & (key_index[None, :] <= query_index[:, None])
            scores = jnp.where(allowed[None], scores, masked_score)
        attn_probs = low(jax.nn.softmax(scores, axis=-1))
        context = jnp.einsum('hqk,khd->qhd', attn_probs, value_heads, precision=highest)
        return context.reshape(block_rows, HEADS * HEAD_DIM)
    blocks = lax.map(jax.checkpoint(one_block), jnp.arange(row_count // block_rows, dtype=jnp.int32))
    return blocks.reshape(row_count, HEADS * HEAD_DIM)

def attention_branch(normed, source, attn_stack, first_slot, vec_table, first_vec, segment_row, causal):
    scale = HEAD_DIM ** (-0.5)
    queries = low(low_back((matmul(normed, attn_stack[first_slot]) + vec_table[first_vec]) * scale))
    keys_out = low(low_back(matmul(source, attn_stack[first_slot + 1])))
    values_out = low(low_back(matmul(source, attn_stack[first_slot + 2]) + vec_table[first_vec + 1]))
    context = low(low_back(attend(queries, keys_out, values_out, segment_row, causal)))
    return low_back(matmul(context, attn_stack[first_slot + 3]) + vec_table[first_vec + 2])

def mlp_branch(normed, up_proj, up_bias, down_proj, down_bias):
    pre_act = low_back(matmul(normed, up_proj) + up_bias)
    hidden = low(jax.nn.gelu(pre_act, approximate=False))
    return low_back(matmul(hidden, down_proj) + down_bias)

def encoder_block(inputs, attn_stack, up_proj, down_proj, vec_table, up_bias):
    normed = low(layer_norm(inputs, vec_table[0], vec_table[1]))
    middle = inputs + attention_branch(normed, normed, attn_stack, 0, vec_table, 2, None, False)
    mlp_normed = low(layer_norm(middle, vec_table[5], vec_table[6]))
    return middle + mlp_branch(mlp_normed, up_proj, up_bias, down_proj, vec_table[7])

def decoder_block(inputs, memory_in, segment_row, attn_stack, up_proj, down_proj, vec_table, up_bias, down_bias):
    normed = low(layer_norm(inputs, vec_table[0], vec_table[1]))
    first_mid = inputs + attention_branch(normed, normed, attn_stack, 0, vec_table, 2, segment_row, True)
    cross_normed = low(layer_norm(first_mid, vec_table[5], vec_table[6]))
    second_mid = first_mid + attention_branch(cross_normed, memory_in, attn_stack, 4, vec_table, 7, None, False)
    mlp_normed = low(layer_norm(second_mid, vec_table[10], vec_table[11]))
    return second_mid + mlp_branch(mlp_normed, up_proj, up_bias, down_proj, down_bias)

def reference(frames, tokens, memory, segment_ids, enc_attn, enc_up, enc_down, enc_vec, enc_up_bias, dec_attn, dec_up, dec_down, dec_vec, dec_up_bias, dec_down_bias, enc_out_grad, dec_out_grad):
    enc_weights = (low(enc_attn), low(enc_up), low(enc_down), low(enc_vec), low(enc_up_bias))
    dec_weights = (low(dec_attn), low(dec_up), low(dec_down), low(dec_vec), low(dec_up_bias), low(dec_down_bias))
    enc_zeros = tuple((jnp.zeros_like(weight) for weight in enc_weights))
    dec_zeros = tuple((jnp.zeros_like(weight) for weight in dec_weights))

    def per_clip(totals, clip_items):
        frame_row, token_row, memory_row, segment_row, enc_cot, dec_cot = clip_items
        enc_value, enc_pull = jax.vjp(encoder_block, frame_row.astype(jnp.float32), *enc_weights)
        enc_parts = enc_pull(enc_cot.astype(jnp.float32))

        def decoder_call(token_in, memory_in, *weights):
            return decoder_block(token_in, memory_in, segment_row, *weights)
        dec_value, dec_pull = jax.vjp(decoder_call, token_row.astype(jnp.float32), memory_row.astype(jnp.float32), *dec_weights)
        dec_parts = dec_pull(dec_cot.astype(jnp.float32))
        enc_totals = tuple((running + part_grad for running, part_grad in zip(totals[0], enc_parts[1:])))
        dec_totals = tuple((running + part_grad for running, part_grad in zip(totals[1], dec_parts[2:])))
        return ((enc_totals, dec_totals), (enc_value, dec_value, enc_parts[0], dec_parts[0], dec_parts[1]))
    sums, stacked = lax.scan(per_clip, (enc_zeros, dec_zeros), (frames, tokens, memory, segment_ids, enc_out_grad, dec_out_grad))
    enc_sums, dec_sums = sums
    enc_out, dec_out, frames_grad, tokens_grad, memory_grad = stacked
    return (enc_out, dec_out, frames_grad, tokens_grad, memory_grad, enc_sums[0], enc_sums[1], enc_sums[2], enc_sums[3], enc_sums[4], dec_sums[0], dec_sums[1], dec_sums[2], dec_sums[3], dec_sums[4], dec_sums[5])
```

```python
import functools

import jax
import jax.numpy as jnp
from jax import lax
from jax.experimental import pallas as pl
from jax.experimental.pallas import tpu as pltpu
from jax.sharding import PartitionSpec as P

HEADS = 12
epsilon = 1e-05
masked_score = -1e30
low = jnp.bfloat16
full = jnp.float32
MIB = 1024 * 1024


def dot_nn(left, right):
    return lax.dot_general(left, right, (((1,), (0,)), ((), ())), preferred_element_type=full)


def dot_nt(left, right):
    return lax.dot_general(left, right, (((1,), (1,)), ((), ())), preferred_element_type=full)


def dot_tn(left, right):
    return lax.dot_general(left, right, (((0,), (0,)), ((), ())), preferred_element_type=full)


def whole(shape):
    return pl.BlockSpec(shape, lambda *_: (0,) * len(shape), pipeline_mode=pl.Buffered(1))


def kept(shape):
    return pl.BlockSpec(shape, lambda *_: (0,) * len(shape))


def rows(count, width):
    return pl.BlockSpec((count, width), lambda i: (i, 0))


def shape_of(shape, kind):
    return jax.ShapeDtypeStruct(shape, kind)


def call(kernel, grid, in_specs, out_specs, out_shape, args, flops, scratch=(), exps=0, limit=48):
    moved = sum(a.size * a.dtype.itemsize for a in args)
    moved += sum(s.size * s.dtype.itemsize for s in out_shape)
    return pl.pallas_call(
        kernel,
        grid=grid,
        in_specs=in_specs,
        out_specs=out_specs,
        out_shape=out_shape,
        scratch_shapes=list(scratch),
        cost_estimate=pl.CostEstimate(
            flops=int(flops), bytes_accessed=int(moved), transcendentals=int(exps)
        ),
        compiler_params=pltpu.CompilerParams(vmem_limit_bytes=limit * MIB),
    )(*args)


def block_of(count):
    return 256 if count % 256 == 0 else count // 2 if (count // 2) % 16 == 0 else count


def spread_of(inputs):
    center = inputs - jnp.mean(inputs, -1, keepdims=True)
    rate = lax.rsqrt(jnp.mean(center * center, -1, keepdims=True) + epsilon)
    return center * rate, rate


def norm_pull(unit, rate, gain, upstream):
    a = upstream * gain
    along = jnp.mean(a * unit, -1, keepdims=True)
    return rate * (a - jnp.mean(a, -1, keepdims=True) - unit * along)


def add_row(ref, row, block):
    ref[pl.ds(row, 1), :] += jnp.sum(block.astype(full), 0, keepdims=True)


def clear_at_start(*refs):
    @pl.when(pl.program_id(0) == 0)
    def _():
        for ref in refs:
            ref[...] = jnp.zeros_like(ref)


def norm_project_kernel(scale, x_ref, vec_ref, wq_ref, wk_ref, wv_ref, n_ref, q_ref, k_ref, v_ref):
    unit, _ = spread_of(x_ref[...].astype(full))
    n = (unit * vec_ref[0:1, :] + vec_ref[1:2, :]).astype(low)
    n_ref[...] = n
    q_ref[...] = ((dot_nn(n, wq_ref[...]) + vec_ref[2:3, :]) * scale).astype(low)
    k_ref[...] = dot_nn(n, wk_ref[...]).astype(low)
    v_ref[...] = (dot_nn(n, wv_ref[...]) + vec_ref[3:4, :]).astype(low)


def norm_project(x, vecs, wq, wk, wv):
    count, width = x.shape
    step = block_of(count)
    out = shape_of((count, width), low)
    return call(
        functools.partial(norm_project_kernel, (width // HEADS) ** -0.5),
        (count // step,),
        [rows(step, width), whole(vecs.shape)] + [whole((width, width))] * 3,
        [rows(step, width)] * 4,
        [out] * 4,
        (x, vecs, wq, wk, wv),
        6 * count * width * width,
    )


def allowed_bias(seg_a, seg_b, a_axis):
    shape = (seg_a.size, seg_b.size)
    first = lax.broadcasted_iota(jnp.int32, shape, 0)
    second = lax.broadcasted_iota(jnp.int32, shape, 1)
    later = second <= first if a_axis == 0 else first <= second
    return jnp.where((seg_a == seg_b) & later, 0.0, masked_score).astype(full)


def attend_kernel(step, masked, *refs):
    if masked:
        q_ref, k_ref, v_ref, col_ref, row_ref, o_ref, sum_ref, hold, bias = refs
    else:
        q_ref, k_ref, v_ref, o_ref, sum_ref, hold = refs
    pair = pl.program_id(0)
    count = q_ref.shape[0]
    lane = lax.broadcasted_iota(jnp.int32, (1, 128), 1)
    k, v = k_ref[...], v_ref[...]

    @pl.when(pair == 0)
    def _():
        hold[...] = jnp.zeros_like(hold)
        if masked:
            bias[...] = allowed_bias(col_ref[...], row_ref[...], 0)

    def one(index, carry):
        start = pl.multiple_of(index * step, step)
        block = q_ref[pl.ds(start, step), :]
        outs = []
        sums = hold[pl.ds(start, step), :]
        for h in range(2):
            mine = (lane < 64) == (h == 0)
            s = dot_nt(jnp.where(mine, block, jnp.zeros_like(block)), k)
            if masked:
                s = s + bias[pl.ds(start, step), :]
            top = jnp.max(s, -1, keepdims=True)
            e = jnp.exp(s - top)
            total = jnp.sum(e, -1, keepdims=True)
            outs.append(dot_nn(e.astype(low), v) / total)
            sums = jnp.where(lane == 2 * pair + h, top + jnp.log(total), sums)
        o_ref[pl.ds(start, step), :] = jnp.where(lane < 64, outs[0], outs[1]).astype(low)
        hold[pl.ds(start, step), :] = sums
        return carry

    lax.fori_loop(0, count // step, one, 0)

    @pl.when(pair == pl.num_programs(0) - 1)
    def _():
        sum_ref[...] = hold[...].T[:16, :]


def attend(q, k, v, seg=None):
    count, width = q.shape
    keys = k.shape[0]
    step = block_of(count)
    pairs = width // 128
    column = lambda n: pl.BlockSpec((n, 128), lambda j: (0, j))
    args, specs = [q, k, v], [column(count), column(keys), column(keys)]
    scratch = [pltpu.VMEM((count, 128), full)]
    if seg is not None:
        args += [seg.reshape(count, 1), seg.reshape(1, count)]
        specs += [whole((count, 1)), whole((1, count))]
        scratch.append(pltpu.VMEM((count, count), full))
    return call(
        functools.partial(attend_kernel, step, seg is not None),
        (pairs,),
        specs,
        [column(count), kept((16, count))],
        [shape_of((count, width), low), shape_of((16, count), full)],
        args,
        8 * 2 * count * keys * width,
        scratch,
        HEADS * count * keys,
    )


def attend_back_kernel(step, masked, scale, *refs):
    if masked:
        q_ref, k_ref, v_ref, o_ref, g_ref, sum_ref, col_ref, row_ref, gq_ref, gk_ref, gv_ref, acc_k, acc_v, dots, bias = refs
    else:
        q_ref, k_ref, v_ref, o_ref, g_ref, sum_ref, gq_ref, gk_ref, gv_ref, acc_k, acc_v, dots = refs
    pair = pl.program_id(0)
    count = q_ref.shape[0]
    lane = lax.broadcasted_iota(jnp.int32, (1, 128), 1)
    k, v = k_ref[...], v_ref[...]
    if masked:

        @pl.when(pair == 0)
        def _():
            bias[...] = allowed_bias(col_ref[...], row_ref[...], 1)

    acc_k[...] = jnp.zeros_like(acc_k)
    acc_v[...] = jnp.zeros_like(acc_v)

    def one(index, carry):
        start = pl.multiple_of(index * step, step)
        span = pl.ds(start, step)
        q, g = q_ref[span, :], g_ref[span, :]
        both = (g.astype(full) * o_ref[span, :].astype(full)).T
        gqs = []
        for h in range(2):
            mine = (lane < 64) == (h == 0)
            qh = jnp.where(mine, q, jnp.zeros_like(q))
            gh = jnp.where(mine, g, jnp.zeros_like(g))
            top = sum_ref[pl.ds(2 * pair + h, 1), span]
            s = dot_nt(k, qh)
            if masked:
                s = s + bias[:, span]
            p = jnp.exp(s - top)
            away = dot_nt(v, gh) - jnp.sum(both[64 * h : 64 * h + 64, :], 0, keepdims=True)
            gs = (p * away).astype(low)
            acc_v[...] += dot_nn(p.astype(low), gh)
            acc_k[...] += dot_nn(gs, qh)
            gqs.append(dot_tn(gs, k))
        gq_ref[span, :] = (jnp.where(lane < 64, gqs[0], gqs[1]) * scale).astype(low)
        return carry

    if count == step:
        one(0, 0)
    else:
        lax.fori_loop(0, count // step, one, 0)
    gk_ref[...] = acc_k[...].astype(low)
    gv_ref[...] = acc_v[...].astype(low)


def attend_back(q, k, v, o, g, sums, seg=None):
    count, width = q.shape
    keys = k.shape[0]
    step = 256 if count % 256 == 0 else count
    pairs = width // 128
    column = lambda n: pl.BlockSpec((n, 128), lambda j: (0, j))
    args = [q, k, v, o, g, sums]
    specs = [column(count), column(keys), column(keys), column(count), column(count), whole((16, count))]
    scratch = [pltpu.VMEM((keys, 128), full), pltpu.VMEM((keys, 128), full), pltpu.VMEM((8, 128), full)]
    if seg is not None:
        args += [seg.reshape(count, 1), seg.reshape(1, count)]
        specs += [whole((count, 1)), whole((1, count))]
        scratch.append(pltpu.VMEM((count, count), full))
    return call(
        functools.partial(attend_back_kernel, step, seg is not None, (width // HEADS) ** -0.5),
        (pairs,),
        specs,
        [column(count), column(keys), column(keys)],
        [shape_of((count, width), low), shape_of((keys, width), low), shape_of((keys, width), low)],
        args,
        20 * 2 * count * keys * width,
        scratch,
        HEADS * count * keys,
    )


def feed_kernel(
    chunk,
    x_ref, o_ref, up_ref, vec_ref, bias_ref, wo_ref, wu_ref, wd_ref,
    out_ref, n_ref, hid_ref, gpre_ref, gr_ref, gmid_ref, grm_ref, go_ref, sums_ref, gbias_ref,
):
    clear_at_start(sums_ref, gbias_ref)
    mid = x_ref[...].astype(full) + dot_nn(o_ref[...], wo_ref[...]) + vec_ref[0:1, :]
    unit, rate = spread_of(mid)
    n = (unit * vec_ref[1:2, :] + vec_ref[2:3, :]).astype(low)
    n_ref[...] = n
    upstream = up_ref[...]
    gr = upstream.astype(low)
    gr_ref[...] = gr
    add_row(sums_ref, 0, gr)
    total = gn = None
    for first in range(0, wu_ref.shape[1], chunk):
        cut = slice(first, first + chunk)
        pre = dot_nn(n, wu_ref[:, cut]) + bias_ref[:, cut]
        half = 0.5 + 0.5 * lax.erf(pre * 0.7071067811865476)
        hid = (pre * half).astype(low)
        slope = half + pre * (0.3989422804014327 * jnp.exp(-0.5 * pre * pre))
        gpre = (dot_nt(gr, wd_ref[cut, :]) * slope).astype(low)
        hid_ref[:, cut] = hid
        gpre_ref[:, cut] = gpre
        gbias_ref[:, cut] += jnp.sum(gpre.astype(full), 0, keepdims=True)
        one, two = dot_nn(hid, wd_ref[cut, :]), dot_nt(gpre, wu_ref[:, cut])
        total = one if total is None else total + one
        gn = two if gn is None else gn + two
    out_ref[...] = mid + total + vec_ref[3:4, :]
    add_row(sums_ref, 1, gn * unit)
    add_row(sums_ref, 2, gn)
    gmid = upstream + norm_pull(unit, rate, vec_ref[1:2, :], gn)
    gmid_ref[...] = gmid
    grm = gmid.astype(low)
    grm_ref[...] = grm
    add_row(sums_ref, 3, grm)
    go_ref[...] = dot_nt(grm, wo_ref[...]).astype(low)


def feed(x, o, upstream, vecs, bias, wo, wu, wd, chunk=768):
    count, width = x.shape
    ff = wu.shape[1]
    step = block_of(count)
    wide, thin = rows(step, ff), rows(step, width)
    return call(
        functools.partial(feed_kernel, chunk),
        (count // step,),
        [thin, thin, thin, whole(vecs.shape), whole(bias.shape), whole(wo.shape), whole(wu.shape), whole(wd.shape)],
        [thin, thin, wide, wide, thin, thin, thin, thin, kept((8, width)), kept((1, ff))],
        [
            shape_of((count, width), full),
            shape_of((count, width), low),
            shape_of((count, ff), low),
            shape_of((count, ff), low),
            shape_of((count, width), low),
            shape_of((count, width), full),
            shape_of((count, width), low),
            shape_of((count, width), low),
            shape_of((8, width), full),
            shape_of((1, ff), full),
        ],
        (x, o, upstream, vecs, bias, wo, wu, wd),
        4 * count * width * width + 8 * count * width * ff,
        exps=2 * count * ff,
        limit=56,
    )


def project_back_kernel(x_ref, up_ref, gq_ref, gk_ref, gv_ref, vec_ref, wq_ref, wk_ref, wv_ref, gx_ref, sums_ref):
    clear_at_start(sums_ref)
    gq, gk, gv = gq_ref[...], gk_ref[...], gv_ref[...]
    gn = dot_nt(gq, wq_ref[...]) + dot_nt(gk, wk_ref[...]) + dot_nt(gv, wv_ref[...])
    unit, rate = spread_of(x_ref[...].astype(full))
    add_row(sums_ref, 0, gn * unit)
    add_row(sums_ref, 1, gn)
    add_row(sums_ref, 2, gq)
    add_row(sums_ref, 3, gv)
    gx_ref[...] = up_ref[...] + norm_pull(unit, rate, vec_ref[0:1, :], gn)


def project_back(x, upstream, gq, gk, gv, vecs, wq, wk, wv):
    count, width = x.shape
    step = block_of(count)
    thin = rows(step, width)
    return call(
        project_back_kernel,
        (count // step,),
        [thin] * 5 + [whole(vecs.shape)] + [whole((width, width))] * 3,
        [thin, kept((8, width))],
        [shape_of((count, width), full), shape_of((8, width), full)],
        (x, upstream, gq, gk, gv, vecs, wq, wk, wv),
        6 * count * width * width,
    )


def bridge_kernel(scale, x_ref, o_ref, vec_ref, wo_ref, wq_ref, mid_ref, n_ref, q_ref):
    mid = x_ref[...].astype(full) + dot_nn(o_ref[...], wo_ref[...]) + vec_ref[0:1, :]
    mid_ref[...] = mid
    unit, _ = spread_of(mid)
    n = (unit * vec_ref[1:2, :] + vec_ref[2:3, :]).astype(low)
    n_ref[...] = n
    q_ref[...] = ((dot_nn(n, wq_ref[...]) + vec_ref[3:4, :]) * scale).astype(low)


def bridge(x, o, vecs, wo, wq):
    count, width = x.shape
    step = block_of(count)
    thin = rows(step, width)
    return call(
        functools.partial(bridge_kernel, (width // HEADS) ** -0.5),
        (count // step,),
        [thin, thin, whole(vecs.shape), whole((width, width)), whole((width, width))],
        [thin] * 3,
        [shape_of((count, width), full), shape_of((count, width), low), shape_of((count, width), low)],
        (x, o, vecs, wo, wq),
        4 * count * width * width,
    )


def bridge_back_kernel(mid_ref, up_ref, gq_ref, vec_ref, wo_ref, wq_ref, g_ref, gr_ref, go_ref, sums_ref):
    clear_at_start(sums_ref)
    gq = gq_ref[...]
    gn = dot_nt(gq, wq_ref[...])
    unit, rate = spread_of(mid_ref[...])
    add_row(sums_ref, 0, gn * unit)
    add_row(sums_ref, 1, gn)
    add_row(sums_ref, 2, gq)
    g = up_ref[...] + norm_pull(unit, rate, vec_ref[1:2, :], gn)
    g_ref[...] = g
    gr = g.astype(low)
    gr_ref[...] = gr
    add_row(sums_ref, 3, gr)
    go_ref[...] = dot_nt(gr, wo_ref[...]).astype(low)


def bridge_back(mid, upstream, gq, vecs, wo, wq):
    count, width = mid.shape
    step = block_of(count)
    thin = rows(step, width)
    return call(
        bridge_back_kernel,
        (count // step,),
        [thin] * 3 + [whole(vecs.shape), whole((width, width)), whole((width, width))],
        [thin] * 3 + [kept((8, width))],
        [
            shape_of((count, width), full),
            shape_of((count, width), low),
            shape_of((count, width), low),
            shape_of((8, width), full),
        ],
        (mid, upstream, gq, vecs, wo, wq),
        4 * count * width * width,
    )


def memory_kernel(s_ref, vec_ref, wk_ref, wv_ref, k_ref, v_ref):
    s = s_ref[...]
    k_ref[...] = dot_nn(s, wk_ref[...]).astype(low)
    v_ref[...] = (dot_nn(s, wv_ref[...]) + vec_ref[0:1, :]).astype(low)


def memory_project(s, vecs, wk, wv):
    count, width = s.shape
    step = block_of(count)
    thin = rows(step, width)
    return call(
        memory_kernel,
        (count // step,),
        [thin, whole(vecs.shape), whole((width, width)), whole((width, width))],
        [thin] * 2,
        [shape_of((count, width), low)] * 2,
        (s, vecs, wk, wv),
        4 * count * width * width,
    )


def memory_back_kernel(gk_ref, gv_ref, wk_ref, wv_ref, g_ref, sums_ref):
    clear_at_start(sums_ref)
    gv = gv_ref[...]
    g_ref[...] = dot_nt(gk_ref[...], wk_ref[...]) + dot_nt(gv, wv_ref[...])
    add_row(sums_ref, 0, gv)


def memory_back(gk, gv, wk, wv):
    count, width = gk.shape
    step = block_of(count)
    thin = rows(step, width)
    return call(
        memory_back_kernel,
        (count // step,),
        [thin] * 2 + [whole((width, width))] * 2,
        [thin, kept((8, width))],
        [shape_of((count, width), full), shape_of((8, width), full)],
        (gk, gv, wk, wv),
        4 * count * width * width,
    )


def weight_grad(left, right):
    return dot_tn(left, right).astype(low)


def eight(*parts):
    table = jnp.concatenate([p.reshape(-1, p.shape[-1]) for p in parts], 0)
    return jnp.pad(table, ((0, 8 - table.shape[0]), (0, 0)))


def encoder(x, weights, upstream):
    wq, wk, wv, wo, wu, wd, vecs, up_bias = weights
    n1, q, k, v = norm_project(x, eight(vecs[0:4]), wq, wk, wv)
    o, sums = attend(q, k, v)
    out, n2, hid, gpre, gr, gmid, grm, go, feed_sums, gbias = feed(
        x, o, upstream, eight(vecs[4:8]), up_bias, wo, wu, wd
    )
    feed_grads = (weight_grad(n2, gpre), weight_grad(hid, gr))
    feed_grads, go = lax.optimization_barrier((feed_grads, go))
    gq, gk, gv = attend_back(q, k, v, o, go, sums)
    gx, first_sums = project_back(x, gmid, gq, gk, gv, eight(vecs[0:2]), wq, wk, wv)
    attn_grads = (
        weight_grad(n1, gq),
        weight_grad(n1, gk),
        weight_grad(n1, gv),
        weight_grad(o, grm),
    )
    vec_grad = jnp.concatenate([first_sums[0:4], feed_sums[3:4], feed_sums[1:3], feed_sums[0:1]], 0)
    return out, gx, attn_grads, feed_grads, vec_grad, gbias


def decoder(y, memory, seg, weights, upstream):
    wq, wk, wv, wo, cq, ck, cv, co, wu, wd, vecs, up_bias, down_bias = weights
    m1, q, k, v = norm_project(y, eight(vecs[0:4]), wq, wk, wv)
    o, sums = attend(q, k, v, seg)
    first, m2, q2 = bridge(y, o, eight(vecs[4:8]), wo, cq)
    k2, v2 = memory_project(memory, eight(vecs[8:9]), ck, cv)
    o2, sums2 = attend(q2, k2, v2)
    out, m3, hid, gpre, gr, gsecond, grs, go2, feed_sums, gbias = feed(
        first, o2, upstream, eight(vecs[9:12], down_bias), up_bias, co, wu, wd
    )
    feed_grads = (weight_grad(m3, gpre), weight_grad(hid, gr))
    feed_grads, go2 = lax.optimization_barrier((feed_grads, go2))
    gq2, gk2, gv2 = attend_back(q2, k2, v2, o2, go2, sums2)
    gmemory, memory_sums = memory_back(gk2, gv2, ck, cv)
    gfirst, grf, go, bridge_sums = bridge_back(first, gsecond, gq2, eight(vecs[4:8]), wo, cq)
    gq, gk, gv = attend_back(q, k, v, o, go, sums, seg)
    gy, first_sums = project_back(y, gfirst, gq, gk, gv, eight(vecs[0:2]), wq, wk, wv)
    attn_grads = (
        weight_grad(m1, gq),
        weight_grad(m1, gk),
        weight_grad(m1, gv),
        weight_grad(o, grf),
        weight_grad(m2, gq2),
        weight_grad(memory, gk2),
        weight_grad(memory, gv2),
        weight_grad(o2, grs),
    )
    vec_grad = jnp.concatenate(
        [
            first_sums[0:4],
            bridge_sums[3:4],
            bridge_sums[0:3],
            memory_sums[0:1],
            feed_sums[3:4],
            feed_sums[1:3],
        ],
        0,
    )
    return out, gy, gmemory, attn_grads, feed_grads, vec_grad, gbias, feed_sums[0:1]


def parts_of(size):
    even = [list(range(k, size, 2)) for k in range(2)]
    swap = [(k, k ^ 1) for k in range(size)]
    return even, swap


def gather_rows(packed, fsdp):
    even, swap = parts_of(fsdp)
    rows, width = packed.shape
    lines = lax.all_gather(packed, "rep", axis=0, tiled=False)
    mine = lax.all_gather(lines, "fsdp", axis=0, tiled=False, axis_index_groups=even)
    other = lax.ppermute(mine, "fsdp", swap)
    first = lax.axis_index("fsdp") % 2 == 0
    whole = jnp.stack([jnp.where(first, mine, other), jnp.where(first, other, mine)], 1)
    return whole.reshape(-1, rows, width)


def scatter_rows(parts, fsdp):
    even, swap = parts_of(fsdp)
    shards, rows, width = parts.shape
    laid = parts.reshape(fsdp // 2, 2, shards // fsdp, rows, width)
    core = lax.axis_index("fsdp") % 2
    theirs = lax.dynamic_index_in_dim(laid, 1 - core, 1, keepdims=False)
    ours = lax.dynamic_index_in_dim(laid, core, 1, keepdims=False)
    one = ours + lax.ppermute(theirs, "fsdp", swap)
    two = lax.psum_scatter(one, "fsdp", scatter_dimension=0, tiled=False, axis_index_groups=even)
    return lax.psum_scatter(two, "rep", scatter_dimension=0, tiled=False)


def slots_of(whole, first, count, own):
    shards, _, width = whole.shape
    part = whole[:, first * own : (first + count) * own].reshape(shards, count, own, width)
    return part.transpose(1, 0, 2, 3).reshape(count, shards * own, width)


def rows_of(slots, shards):
    count, total, width = slots.shape
    own = total // shards
    part = slots.astype(jnp.bfloat16).reshape(count, shards, own, width)
    return part.transpose(1, 0, 2, 3).reshape(shards, count * own, width)


def columns_to_slots(up):
    rows, columns = up.shape
    return up.reshape(rows, columns // 768, 768).transpose(1, 0, 2)


def body(
    fsdp,
    rep,
    frames,
    tokens,
    memory,
    segment_ids,
    enc_attn,
    enc_up,
    enc_down,
    enc_vec,
    enc_up_bias,
    dec_attn,
    dec_up,
    dec_down,
    dec_vec,
    dec_up_bias,
    dec_down_bias,
    enc_out_grad,
    dec_out_grad,
):
    shards = fsdp * rep
    own = enc_attn.shape[1]
    width = enc_attn.shape[2]
    ff = enc_up.shape[1]
    wide = ff // width

    def pack(attn, up, down):
        low = [attn.astype(jnp.bfloat16).reshape(-1, width)]
        if up is not None:
            low.append(columns_to_slots(up.astype(jnp.bfloat16)).reshape(-1, width))
            low.append(down.astype(jnp.bfloat16))
        return jnp.concatenate(low, 0)

    def unpack(whole, slots):
        attn = slots_of(whole, 0, slots, own)
        up = slots_of(whole, slots, wide, own).transpose(1, 0, 2).reshape(width, ff)
        down = whole[:, (slots + wide) * own :].reshape(ff, width)
        return attn, up, down

    small = jnp.concatenate(
        [
            enc_vec.reshape(-1),
            dec_vec.reshape(-1),
            enc_up_bias,
            dec_up_bias,
            dec_down_bias,
        ]
    ).astype(jnp.bfloat16)
    small_all = lax.all_gather(small, ("fsdp", "rep"), axis=0, tiled=False)
    cuts = [8 * own, 12 * own, wide * own, wide * own, own]
    edges = [sum(cuts[:k]) for k in range(6)]
    piece = [small_all[:, edges[k] : edges[k + 1]] for k in range(5)]
    enc_vec_w = piece[0].reshape(shards, 8, own).transpose(1, 0, 2).reshape(8, width)
    dec_vec_w = piece[1].reshape(shards, 12, own).transpose(1, 0, 2).reshape(12, width)
    enc_bias_w = piece[2].reshape(ff)
    dec_bias_w = piece[3].reshape(ff)
    dec_down_bias_w = piece[4].reshape(width)

    enc_whole = gather_rows(pack(enc_attn, enc_up, enc_down), fsdp)
    dec_whole = gather_rows(pack(dec_attn, dec_up, dec_down), fsdp)
    enc_attn_w, enc_up_w, enc_down_w = unpack(enc_whole, 4)
    dec_attn_w, dec_up_w, dec_down_w = unpack(dec_whole, 8)
    enc_weights = (enc_attn_w, enc_up_w, enc_down_w, enc_vec_w, enc_bias_w)
    dec_weights = (dec_attn_w, dec_up_w, dec_down_w, dec_vec_w, dec_bias_w, dec_down_bias_w)

    enc_set = tuple(enc_attn_w[k] for k in range(4)) + (
        enc_up_w,
        enc_down_w,
        enc_vec_w.astype(full),
        enc_bias_w.astype(full)[None],
    )
    dec_set = tuple(dec_attn_w[k] for k in range(8)) + (
        dec_up_w,
        dec_down_w,
        dec_vec_w.astype(full),
        dec_bias_w.astype(full)[None],
        dec_down_bias_w.astype(full)[None],
    )

    def reduce_feed(grads):
        up_rows = rows_of(columns_to_slots(grads[0]), shards)
        down_rows = grads[1].reshape(shards, -1, width)
        mine = scatter_rows(jnp.concatenate([up_rows, down_rows], 1), fsdp).astype(full)
        up_mine = mine[: wide * own].reshape(wide, own, width).transpose(1, 0, 2).reshape(own, ff)
        return up_mine, mine[wide * own :]

    def reduce_attn(grads):
        parts = jnp.concatenate([g.reshape(shards, own, width) for g in grads], 1)
        return scatter_rows(parts, fsdp).astype(full).reshape(-1, own, width)

    enc_result, frames_grad, enc_attn_g, enc_feed_g, enc_vec_g, enc_bias_g = encoder(
        frames[0], enc_set, enc_out_grad[0]
    )
    enc_up_grad, enc_down_grad = reduce_feed(enc_feed_g)
    enc_attn_grad = reduce_attn(enc_attn_g)
    token_rows, frames_grad = lax.optimization_barrier((tokens[0], frames_grad))
    (
        dec_result,
        tokens_grad,
        memory_grad,
        dec_attn_g,
        dec_feed_g,
        dec_vec_g,
        dec_bias_g,
        dec_down_bias_g,
    ) = decoder(token_rows, memory[0], segment_ids[0], dec_set, dec_out_grad[0])
    dec_up_grad, dec_down_grad = reduce_feed(dec_feed_g)
    dec_attn_grad = reduce_attn(dec_attn_g)

    def by_owner(table):
        count = table.shape[0]
        return table.reshape(count, shards, -1).transpose(1, 0, 2).reshape(shards, -1)

    small_grad = jnp.concatenate(
        [
            by_owner(enc_vec_g),
            by_owner(dec_vec_g),
            by_owner(enc_bias_g),
            by_owner(dec_bias_g),
            by_owner(dec_down_bias_g),
        ],
        1,
    )
    spare = -small_grad.shape[1] % 1024
    small_grad = jnp.pad(small_grad, ((0, 0), (0, spare))).reshape(shards, -1, 128)
    small_mine = lax.psum_scatter(
        small_grad, ("fsdp", "rep"), scatter_dimension=0, tiled=False
    ).reshape(-1)
    take = [small_mine[edges[k] : edges[k + 1]] for k in range(5)]
    return (
        enc_result[None],
        dec_result[None],
        frames_grad[None],
        tokens_grad[None],
        memory_grad[None],
        enc_attn_grad,
        enc_up_grad,
        enc_down_grad,
        take[0].reshape(8, own),
        take[2],
        dec_attn_grad,
        dec_up_grad,
        dec_down_grad,
        take[1].reshape(12, own),
        take[3],
        take[4],
    )


def solution(mesh):
    placed = (
        P(("fsdp", "rep"), None, None),
        P(("fsdp", "rep"), None, None),
        P(("fsdp", "rep"), None, None),
        P(("fsdp", "rep"), None),
        P(None, ("fsdp", "rep"), None),
        P(("fsdp", "rep"), None),
        P(("fsdp", "rep"), None),
        P(None, ("fsdp", "rep")),
        P(("fsdp", "rep")),
        P(None, ("fsdp", "rep"), None),
        P(("fsdp", "rep"), None),
        P(("fsdp", "rep"), None),
        P(None, ("fsdp", "rep")),
        P(("fsdp", "rep")),
        P(("fsdp", "rep")),
        P(("fsdp", "rep"), None, None),
        P(("fsdp", "rep"), None, None),
    )
    return jax.shard_map(
        functools.partial(body, mesh.shape["fsdp"], mesh.shape["rep"]),
        mesh=mesh,
        in_specs=placed,
        out_specs=(
            P(("fsdp", "rep"), None, None),
            P(("fsdp", "rep"), None, None),
            P(("fsdp", "rep"), None, None),
            P(("fsdp", "rep"), None, None),
            P(("fsdp", "rep"), None, None),
            P(None, ("fsdp", "rep"), None),
            P(("fsdp", "rep"), None),
            P(("fsdp", "rep"), None),
            P(None, ("fsdp", "rep")),
            P(("fsdp", "rep")),
            P(None, ("fsdp", "rep"), None),
            P(("fsdp", "rep"), None),
            P(("fsdp", "rep"), None),
            P(None, ("fsdp", "rep")),
            P(("fsdp", "rep")),
            P(("fsdp", "rep")),
        ),
        check_vma=False,
    )
```
